32 devices in a mesh: samp: 8 (over y, x, core), blk: 4 (over z).
Axes of the slice: x: 2, y: 2, z: 4, core: 2. Of those that a mesh axis runs over, the one named last changes fastest.
Arguments:
- genotypes: int32 [16384, 6144], P('samp', 'blk'), may hold values from 0 to 2
- phenotype: float32 [16384], P('samp'), may hold values from -15 to 15
- fold_ids: int32 [16384], P('samp'), may hold values from 0 to 4, as said below
Outputs:
- coeff_all: float32 [6144, 400], P('blk')
- fold_scores: float32 [2, 400], replicated
The draws below stay inside these ranges and needn't reach their ends.
Inputs may be any that keep to these rules, and one draw needn't show every extreme that they name: `fold_ids`: every fold holds 3276 or 3277 people.
All inputs are finite; a program needn't handle non-finite values.
Results may differ from the reference program's by a relative error of at most 0.0003.
Values sent between devices are 32-bit elements; how exact they have to be, the bound alone decides.
A program may use at most 128 MiB of HBM per device.

```python
import math
import jax
import jax.numpy as jnp
from jax import lax

BLOCK = 1536
FOLDS = 5
LAMBDAS = 20
SWEEPS = 3
GRID = 400
NSAMP = 16384
NSNP = 6144


def draw_genotypes(key, part):
    freq_key, first_key, second_key = jax.random.split(key, 3)
    frequency = jax.random.randint(freq_key, (NSNP,), 51, 513, dtype=jnp.int32)
    first_copy = jax.random.randint(first_key, (NSAMP, NSNP), 0, 1024, dtype=jnp.int32) < frequency[None, :]
    second_copy = jax.random.randint(second_key, (NSAMP, NSNP), 0, 1024, dtype=jnp.int32) < frequency[None, :]
    return first_copy.astype(jnp.int32) + second_copy.astype(jnp.int32)


def draw_phenotype(key, part):
    row_scale = 1.0 + 2.0 * jnp.arange(NSAMP, dtype=jnp.float32) / (NSAMP - 1)
    normal_part = jnp.clip(jax.random.normal(key, (NSAMP,), jnp.float32), -5.0, 5.0)
    return (normal_part * row_scale).astype(jnp.float32)


def draw_fold_ids(key, part):
    return (jax.random.permutation(key, NSAMP) % FOLDS).astype(jnp.int32)


def setup_inputs(seed: int = 0) -> dict:
    key_of = jax.random.split(jax.random.key(seed), 4)
    return {
        "genotypes": draw_genotypes(jax.random.fold_in(key_of[3], 71), 0),
        "phenotype": draw_phenotype(jax.random.fold_in(key_of[3], 71), 0),
        "fold_ids": draw_fold_ids(jax.random.fold_in(key_of[3], 71), 0),
    }


step_size = 0.6
epsilon = 1e-05
lambda_base = 0.1
lambda_ratio = 1.2
shrink_unit = 0.2
highest = lax.Precision.HIGHEST

def grid_tables():
    column = jnp.arange(GRID)
    fold_of = column % FOLDS
    levels = column // FOLDS % LAMBDAS
    penalty = lambda_base * jnp.exp(levels.astype(jnp.float32) * math.log(lambda_ratio))
    shrink = shrink_unit * (column // (FOLDS * LAMBDAS) + 1).astype(jnp.float32)
    return (fold_of, penalty, shrink)

def soft_threshold(values, cutoff):
    return values - jnp.clip(values, -cutoff, cutoff)

def reference(genotypes, phenotype, fold_ids):
    sample_count = genotypes.shape[0]
    snp_total = genotypes.shape[1]
    dosage = genotypes.astype(jnp.float32)
    onehot = fold_ids[:, None] == jnp.arange(FOLDS)[None, :]
    pheno_split = jnp.where(onehot, phenotype[:, None], 0.0).astype(jnp.float32)
    geno_sum = lax.optimization_barrier(jnp.sum(genotypes, axis=0)).astype(jnp.float32)
    geno_sq = lax.optimization_barrier(jnp.sum(genotypes * genotypes, axis=0)).astype(jnp.float32)
    fold_count = lax.optimization_barrier(jnp.sum(onehot.astype(jnp.int32), axis=0)).astype(jnp.float32)
    fold_pheno_sum = lax.optimization_barrier(jnp.sum(pheno_split, axis=0))
    geno_pheno = jnp.dot(pheno_split.T, dosage, precision=highest)
    snp_mean = geno_sum / sample_count
    scales = jnp.sqrt(geno_sq / sample_count - snp_mean * snp_mean + epsilon)
    train_geno = lax.optimization_barrier(jnp.sum(geno_pheno, axis=0))[None, :] - geno_pheno
    train_pheno = jnp.sum(fold_pheno_sum) - fold_pheno_sum
    zscore = (train_geno - train_pheno[:, None] * snp_mean[None, :]) / (scales[None, :] * jnp.sqrt(sample_count - fold_count)[:, None])
    fold_of, penalty, shrink = grid_tables()
    target_all = zscore.T[:, fold_of]
    predicted = jnp.zeros((sample_count, GRID), jnp.float32)
    coeff_list = []
    for block_idx in range(snp_total // BLOCK):
        low_col = block_idx * BLOCK
        dose_block = dosage[:, low_col:low_col + BLOCK]
        gram_sum = jnp.dot(dose_block.T, dose_block, precision=highest)
        mean_block = snp_mean[low_col:low_col + BLOCK]
        scale_block = scales[low_col:low_col + BLOCK]
        ld_block = (gram_sum / sample_count - mean_block[:, None] * mean_block[None, :]) / (scale_block[:, None] * scale_block[None, :])
        target = target_all[low_col:low_col + BLOCK]
        coeffs = jnp.zeros((BLOCK, GRID), jnp.float32)
        for sweep_idx in range(SWEEPS):
            gradient = (1.0 - shrink) * jnp.dot(ld_block, coeffs, precision=highest) + shrink * coeffs - target
            coeffs = soft_threshold(coeffs - step_size * gradient, step_size * penalty)
        weighted = lax.optimization_barrier((coeffs / scale_block[:, None]).astype(jnp.bfloat16)).astype(jnp.float32)
        predicted = predicted + (jnp.dot(dose_block, weighted, precision=highest) - jnp.dot(mean_block[None, :], weighted, precision=highest))
        coeff_list.append(coeffs)
    predicted = predicted / math.sqrt(snp_total)
    chosen = fold_ids[:, None] == fold_of[None, :]
    numerator = lax.optimization_barrier(jnp.sum(jnp.where(chosen, predicted * phenotype[:, None], 0.0), axis=0))
    denominator = lax.optimization_barrier(jnp.sum(jnp.where(chosen, predicted * predicted, 0.0), axis=0))
    counts = fold_count[fold_of]
    fold_scores = jnp.stack([numerator / counts, denominator / counts])
    return (jnp.concatenate(coeff_list, axis=0), fold_scores)
```

```python
import functools
import math

import jax
import jax.numpy as jnp
from jax import lax
from jax.experimental import pallas as pl
from jax.experimental.pallas import tpu as pltpu
from jax.sharding import PartitionSpec as P

FOLDS = 5
LAMBDAS = 20
SWEEPS = 3
GRID = 400
PER_FOLD = GRID // FOLDS

step_size = 0.6
epsilon = 1e-05
lambda_base = 0.1
lambda_ratio = 1.2
shrink_unit = 0.2
highest = lax.Precision.HIGHEST
MESH = pl.DeviceIdType.MESH


def grid_tables():
    column = jnp.arange(GRID)
    fold_of = column % FOLDS
    levels = column // FOLDS % LAMBDAS
    penalty = lambda_base * jnp.exp(levels.astype(jnp.float32) * math.log(lambda_ratio))
    shrink = shrink_unit * (column // (FOLDS * LAMBDAS) + 1).astype(jnp.float32)
    return (fold_of, penalty, shrink)


def soft_threshold(values, cutoff):
    return values - jnp.clip(values, -cutoff, cutoff)


def flip(index, mask):
    out = index
    for bit in range(mask.bit_length()):
        if mask >> bit & 1:
            out = out + (1 - 2 * (index // (1 << bit) % 2)) * (1 << bit)
    return out


def masks_over(bits):
    out = [0]
    for bit in bits:
        out = out + [m | 1 << bit for m in out]
    return out


def scatter_orders(num):
    bits = num.bit_length() - 1
    return ([0] + list(range(1, bits)), [0] + list(range(bits - 1, 0, -1)))


def scatter_plan(num):
    plan = []
    for order in scatter_orders(num):
        stages = []
        for t in range(len(order)):
            rest = order[t + 1 :]
            got = masks_over(rest)
            got.sort(key=lambda m: tuple(-(m >> b & 1) for b in rest))
            stages.append((order[t], got))
        plan.append(stages)
    return plan


def gather_plan(num):
    plan = []
    for order in scatter_orders(num):
        order = order[::-1]
        plan.append([(bit, masks_over(order[:t])) for t, bit in enumerate(order)])
    return plan


def split3(x):
    hi = x.astype(jnp.bfloat16)
    rest = x - hi.astype(jnp.float32)
    mid = rest.astype(jnp.bfloat16)
    low = (rest - mid.astype(jnp.float32)).astype(jnp.bfloat16)
    return hi, mid, low


def kernel(
    num,
    nblk,
    sample_count,
    snp_total,
    gram,
    dosage,
    pheno_row,
    fold_row,
    pheno_parts,
    fold_parts,
    table,
    perm,
    coeff_out,
    score_out,
    rs_buf,
    stat_buf,
    col_ref,
    target_ref,
    c1_ref,
    c2_ref,
    ld_ref,
    wt_ref,
    sel_buf,
    sel_recv,
    fin_samp,
    fin_blk,
    rs_send,
    rs_recv,
    stat_send,
    stat_recv,
    ag_send,
    ag_recv,
    sel_send,
    sel_rsem,
    fin_send,
    fin_rsem,
    fbl_send,
    fbl_rsem,
):
    me = lax.axis_index("samp")
    zz = lax.axis_index("blk")
    width = gram.shape[0]
    rows = width // num
    half = width // 2

    barrier = pltpu.get_barrier_semaphore()
    for e in range(1, num):
        pl.semaphore_signal(barrier, inc=1, device_id={"samp": flip(me, e)}, device_id_type=MESH)
    for k in range(1, nblk):
        pl.semaphore_signal(
            barrier, inc=1, device_id={"blk": lax.rem(zz + k, nblk)}, device_id_type=MESH
        )
    pl.semaphore_wait(barrier, num - 1 + nblk - 1)

    plan = scatter_plan(num)
    slot_of = {}
    for h in range(2):
        for t, (_, got) in enumerate(plan[h]):
            for e in got:
                slot_of[h, t, e] = len(slot_of)

    def gram_block(e, h):
        return gram.at[pl.ds(pl.multiple_of(flip(me, e) * rows, rows), rows), pl.ds(h * half, half)]

    def rs_copy(h, t, got):
        bit = plan[h][t][0]
        sent = got | 1 << bit
        src = gram_block(sent, h) if t == 0 else rs_buf.at[slot_of[h, t - 1, sent]]
        slot = slot_of[h, t, got]
        return pltpu.make_async_remote_copy(
            src_ref=src,
            dst_ref=rs_buf.at[slot],
            send_sem=rs_send.at[slot],
            recv_sem=rs_recv.at[slot],
            device_id={"samp": flip(me, 1 << bit)},
            device_id_type=MESH,
        )

    stages = len(plan[0])
    for pos in range(len(plan[0][0][1])):
        for h in range(2):
            rs_copy(h, 0, plan[h][0][1][pos]).start()

    pheno = pheno_row[...]
    fold = fold_row[...]
    pieces = [jnp.ones(pheno.shape, jnp.bfloat16).astype(jnp.float32)]
    masked = [jnp.where(fold == k, pheno, 0.0) for k in range(FOLDS)]
    parts = [split3(x) for x in masked]
    for which in range(3):
        for k in range(FOLDS):
            pieces.append(parts[k][which].astype(jnp.float32))
    left = jnp.concatenate(pieces, axis=0).astype(jnp.bfloat16)
    geno = dosage[...]
    prod = jnp.dot(left, geno, preferred_element_type=jnp.float32)
    squares = jnp.dot(
        jnp.ones((16, geno.shape[0]), jnp.bfloat16), geno * geno, preferred_element_type=jnp.float32
    )
    lane = lax.broadcasted_iota(jnp.int32, (1, width), 1)
    extra = jnp.zeros((1, width), jnp.float32)
    for k in range(FOLDS):
        extra = jnp.where(lane == k, jnp.sum(masked[k], axis=1, keepdims=True), extra)
        count = jnp.sum(jnp.where(fold == k, 1.0, 0.0), axis=1, keepdims=True)
        extra = jnp.where(lane == 8 + k, count, extra)
    stat_buf[me] = jnp.concatenate(
        [
            prod[0:1],
            squares[0:1],
            (prod[1 + 2 * FOLDS : 1 + 3 * FOLDS] + prod[1 + FOLDS : 1 + 2 * FOLDS])
            + prod[1 : 1 + FOLDS],
            extra,
        ],
        axis=0,
    )

    def to_samp(buf, e, send, recv, holder):
        return pltpu.make_async_remote_copy(
            src_ref=buf.at[holder],
            dst_ref=buf.at[holder],
            send_sem=send.at[e - 1],
            recv_sem=recv.at[e - 1],
            device_id={"samp": flip(me, e)},
            device_id_type=MESH,
        )

    for e in range(1, num):
        to_samp(stat_buf, e, stat_send, stat_recv, me).start()

    def rs_stage(t):
        for pos in range(len(plan[0][t][1])):
            for h in range(2):
                got = plan[h][t][1][pos]
                slot = slot_of[h, t, got]
                rs_copy(h, t, got).wait_recv()
                prev = gram_block(got, h) if t == 0 else rs_buf.at[slot_of[h, t - 1, got]]
                rs_buf[slot] = rs_buf[slot] + prev[...]
                if t + 1 < stages and got >> plan[h][t + 1][0] & 1:
                    rs_copy(h, t + 1, got & ~(1 << plan[h][t + 1][0])).start()

    rs_stage(0)

    for e in range(1, num):
        to_samp(stat_buf, e, stat_send, stat_recv, flip(me, e)).wait_recv()
    total = stat_buf[0]
    for d in range(1, num):
        total = total + stat_buf[d]
    mean_row = total[0:1] / sample_count
    scale_row = jnp.sqrt(total[1:2] / sample_count - mean_row * mean_row + epsilon)
    turned = total.T
    mean_col = turned[:, 0:1] / sample_count
    scale_col = jnp.sqrt(turned[:, 1:2] / sample_count - mean_col * mean_col + epsilon)
    col_ref[:, 0:1] = mean_col
    col_ref[:, 1:2] = scale_col
    fold_pheno = [total[7:8, k : k + 1] for k in range(FOLDS)]
    counts = [total[7:8, 8 + k : 9 + k] for k in range(FOLDS)]
    pheno_all = sum(fold_pheno[1:], fold_pheno[0])
    geno_pheno = [turned[:, 2 + k : 3 + k] for k in range(FOLDS)]
    geno_pheno_all = sum(geno_pheno[1:], geno_pheno[0])
    thresh = table[0:1, :]
    shrink = table[1:2, :]
    fold_of = table[2:3, :]
    target = jnp.zeros((width, GRID), jnp.float32)
    for k in range(FOLDS):
        z = (geno_pheno_all - geno_pheno[k] - (pheno_all - fold_pheno[k]) * mean_col) / (
            scale_col * jnp.sqrt(sample_count - counts[k])
        )
        target = jnp.where(fold_of == float(k), z, target)
    target_ref[...] = target
    c1_ref[...] = soft_threshold(step_size * target, thresh)

    for t in range(1, stages):
        rs_stage(t)

    mine = pl.ds(pl.multiple_of(me * rows, rows), rows)
    mean_mine = col_ref[mine, 0:1]
    scale_mine = col_ref[mine, 1:2]
    for h in range(2):
        cols = slice(h * half, (h + 1) * half)
        summed = rs_buf[slot_of[h, stages - 1, 0]]
        ld_ref[:, cols] = (summed / sample_count - mean_mine * mean_row[:, cols]) / (
            scale_mine * scale_row[:, cols]
        )

    def sweep(full, out):
        held = full[mine, :]
        gradient = (
            (1.0 - shrink)
            * jnp.dot(ld_ref[...], full[...], precision=highest, preferred_element_type=jnp.float32)
            + shrink * held
            - target_ref[mine, :]
        )
        out[mine, :] = soft_threshold(held - step_size * gradient, thresh)

    aplan = gather_plan(num)
    aslot = {}
    for h in range(2):
        for t, (_, held) in enumerate(aplan[h]):
            for e in held:
                aslot[h, t, e] = len(aslot)
    part = rows // 2

    def ag_copy(buf, which, h, t, e, owner):
        place = buf.at[pl.ds(pl.multiple_of(owner * rows + h * part, part), part), :]
        slot = aslot[h, t, e]
        return pltpu.make_async_remote_copy(
            src_ref=place,
            dst_ref=place,
            send_sem=ag_send.at[which, slot],
            recv_sem=ag_recv.at[which, slot],
            device_id={"samp": flip(me, 1 << aplan[h][t][0])},
            device_id_type=MESH,
        )

    def gather(buf, which):
        def arrived(h, first, e):
            for t in range(first, len(aplan[h])):
                ag_copy(buf, which, h, t, e, flip(me, e)).start()

        for h in range(2):
            arrived(h, 0, 0)
        for t in range(len(aplan[0])):
            for pos in range(len(aplan[0][t][1])):
                for h in range(2):
                    bit, held = aplan[h][t]
                    e = held[pos]
                    got = e | 1 << bit
                    ag_copy(buf, which, h, t, e, flip(me, got)).wait_recv()
                    arrived(h, t + 1, got)

    def gather_end(buf, which):
        for h in range(2):
            for t, (_, held) in enumerate(aplan[h]):
                for e in held:
                    ag_copy(buf, which, h, t, e, flip(me, e)).wait_send()

    sweep(c1_ref, c2_ref)
    gather(c2_ref, 0)
    sweep(c2_ref, coeff_out)
    gather(coeff_out, 1)

    weighted = (coeff_out[...] / col_ref[:, 1:2]).astype(jnp.bfloat16)
    turned_w = lax.dot_general(
        perm[...], weighted, (((1,), (1,)), ((), ())), preferred_element_type=jnp.float32
    )
    wt_ref[...] = turned_w.astype(jnp.bfloat16)
    offset = jnp.sum(turned_w * mean_row, axis=1, keepdims=True)

    people = fold_parts.shape[2]

    def sel_copy(k):
        return pltpu.make_async_remote_copy(
            src_ref=sel_buf.at[k],
            dst_ref=sel_recv.at[k - 1],
            send_sem=sel_send.at[k - 1],
            recv_sem=sel_rsem.at[k - 1],
            device_id={"blk": lax.rem(zz + k, nblk)},
            device_id_type=MESH,
        )

    for k in list(range(1, nblk)) + [0]:
        peer = lax.rem(zz + k, nblk)
        some = dosage[pl.ds(pl.multiple_of(peer * people, people), people), :]
        value = (
            lax.dot_general(
                wt_ref[...], some, (((1,), (1,)), ((), ())), preferred_element_type=jnp.float32
            )
            - offset
        )
        ids = fold_parts[peer]
        chosen = jnp.zeros((PER_FOLD, people), jnp.float32)
        for f in range(FOLDS):
            chosen = jnp.where(ids == f, value[f * PER_FOLD : (f + 1) * PER_FOLD], chosen)
        sel_buf[k] = chosen
        if k:
            sel_copy(k).start()
    predicted = sel_buf[0]
    for k in range(1, nblk):
        sel_copy(k).wait_recv()
        predicted = predicted + sel_recv[k - 1]
    predicted = predicted / math.sqrt(snp_total)
    ids = fold_parts[zz]
    in_fold = lax.broadcasted_iota(jnp.int32, (8, people), 0) == ids
    lanes = (((1,), (1,)), ((), ()))
    numer = lax.dot_general(
        jnp.where(in_fold, pheno_parts[zz], 0.0),
        predicted,
        lanes,
        precision=highest,
        preferred_element_type=jnp.float32,
    )
    denom = lax.dot_general(
        jnp.where(in_fold, 1.0, 0.0),
        predicted * predicted,
        lanes,
        precision=highest,
        preferred_element_type=jnp.float32,
    )
    both = jnp.concatenate([numer, denom], axis=0)
    fin_samp[me] = jnp.concatenate(
        [both, jnp.zeros((16, fin_samp.shape[2] - PER_FOLD), jnp.float32)], axis=1
    )
    for e in range(1, num):
        to_samp(fin_samp, e, fin_send, fin_rsem, me).start()
    for e in range(1, num):
        to_samp(fin_samp, e, fin_send, fin_rsem, flip(me, e)).wait_recv()
    both = fin_samp[0]
    for d in range(1, num):
        both = both + fin_samp[d]
    fin_blk[zz] = both

    def fbl_copy(k, holder):
        return pltpu.make_async_remote_copy(
            src_ref=fin_blk.at[holder],
            dst_ref=fin_blk.at[holder],
            send_sem=fbl_send.at[k - 1],
            recv_sem=fbl_rsem.at[k - 1],
            device_id={"blk": lax.rem(zz + k, nblk)},
            device_id_type=MESH,
        )

    for k in range(1, nblk):
        fbl_copy(k, zz).start()
    for k in range(1, nblk):
        fbl_copy(k, lax.rem(zz + nblk - k, nblk)).wait_recv()
    both = fin_blk[0]
    for d in range(1, nblk):
        both = both + fin_blk[d]
    row = lax.broadcasted_iota(jnp.int32, (16, 1), 0)
    count_col = jnp.ones((16, 1), jnp.float32)
    for k in range(FOLDS):
        count_col = jnp.where((row == k) | (row == 8 + k), counts[k], count_col)
    score_out[...] = both / count_col

    for h in range(2):
        for t in range(stages):
            for got in plan[h][t][1]:
                rs_copy(h, t, got).wait_send()
    for e in range(1, num):
        to_samp(stat_buf, e, stat_send, stat_recv, me).wait_send()
        to_samp(fin_samp, e, fin_send, fin_rsem, me).wait_send()
    gather_end(c2_ref, 0)
    gather_end(coeff_out, 1)
    for k in range(1, nblk):
        sel_copy(k).wait_send()
        fbl_copy(k, zz).wait_send()


def local(genotypes, phenotype, fold_ids):
    num_rows, width = genotypes.shape
    num = lax.axis_size("samp")
    nblk = lax.axis_size("blk")
    people = num_rows // nblk
    rows = width // num
    dosage = genotypes.astype(jnp.bfloat16)
    gram = jnp.dot(dosage.T, dosage, preferred_element_type=jnp.float32)
    fold_of, penalty, shrink = grid_tables()
    table = jnp.concatenate(
        [
            jnp.stack([step_size * penalty, shrink, fold_of.astype(jnp.float32)]),
            jnp.zeros((5, GRID), jnp.float32),
        ]
    )
    order = jnp.arange(GRID)
    perm = (
        (order % PER_FOLD * FOLDS + order // PER_FOLD)[:, None] == order[None, :]
    ).astype(jnp.bfloat16)
    rs_slots = 2 * (num - 1)
    ag_slots = 2 * (num - 1)
    dma = pltpu.SemaphoreType.DMA
    f32 = jnp.float32
    coeff_all, scores = pl.pallas_call(
        functools.partial(kernel, num, nblk, num_rows * num, width * nblk),
        out_shape=(
            jax.ShapeDtypeStruct((width, GRID), f32),
            jax.ShapeDtypeStruct((16, 128), f32),
        ),
        in_specs=[pl.BlockSpec(memory_space=pltpu.VMEM)] * 8,
        out_specs=(pl.BlockSpec(memory_space=pltpu.VMEM),) * 2,
        scratch_shapes=[
            pltpu.VMEM((rs_slots, rows, width // 2), f32),
            pltpu.VMEM((num, 8, width), f32),
            pltpu.VMEM((width, 8), f32),
            pltpu.VMEM((width, GRID), f32),
            pltpu.VMEM((width, GRID), f32),
            pltpu.VMEM((width, GRID), f32),
            pltpu.VMEM((rows, width), f32),
            pltpu.VMEM((GRID, width), jnp.bfloat16),
            pltpu.VMEM((nblk, PER_FOLD, people), f32),
            pltpu.VMEM((nblk - 1, PER_FOLD, people), f32),
            pltpu.VMEM((num, 16, 128), f32),
            pltpu.VMEM((nblk, 16, 128), f32),
            dma((rs_slots,)),
            dma((rs_slots,)),
            dma((num - 1,)),
            dma((num - 1,)),
            dma((2, ag_slots)),
            dma((2, ag_slots)),
            dma((nblk - 1,)),
            dma((nblk - 1,)),
            dma((num - 1,)),
            dma((num - 1,)),
            dma((nblk - 1,)),
            dma((nblk - 1,)),
        ],
        compiler_params=pltpu.CompilerParams(
            collective_id=0, has_side_effects=True, vmem_limit_bytes=62 * 1024 * 1024
        ),
    )(
        gram,
        dosage,
        phenotype.reshape(1, num_rows),
        fold_ids.reshape(1, num_rows),
        phenotype.reshape(nblk, 1, people),
        fold_ids.reshape(nblk, 1, people),
        table,
        perm,
    )
    scores = scores.reshape(2, 8, 128)[:, :FOLDS, :PER_FOLD]
    return (coeff_all, scores.transpose(0, 2, 1).reshape(2, GRID))


def solution(mesh):
    return jax.shard_map(
        local,
        mesh=mesh,
        in_specs=(P("samp", "blk"), P("samp"), P("samp")),
        out_specs=(P("blk", None), P()),
        check_vma=False,
    )
```

```python
import functools
import math

import jax
import jax.numpy as jnp
import numpy as np
from jax import lax
from jax.experimental import pallas as pl
from jax.experimental.pallas import tpu as pltpu
from jax.sharding import PartitionSpec as P

FOLDS = 5
LAMBDAS = 20
SWEEPS = 3
GRID = 400
PER_FOLD = GRID // FOLDS

step_size = 0.6
epsilon = 1e-05
lambda_base = 0.1
lambda_ratio = 1.2
shrink_unit = 0.2
highest = lax.Precision.HIGHEST
MESH = pl.DeviceIdType.MESH


def grid_tables():
    column = np.arange(GRID)
    fold_of = column % FOLDS
    levels = column // FOLDS % LAMBDAS
    penalty = lambda_base * np.exp(levels * math.log(lambda_ratio))
    shrink = shrink_unit * (column // (FOLDS * LAMBDAS) + 1)
    return (fold_of, penalty, shrink)


def soft_threshold(values, cutoff):
    return values - jnp.clip(values, -cutoff, cutoff)


def flip(index, mask):
    out = index
    for bit in range(mask.bit_length()):
        if mask >> bit & 1:
            out = out + (1 - 2 * (index // (1 << bit) % 2)) * (1 << bit)
    return out


def masks_over(bits):
    out = [0]
    for bit in bits:
        out = out + [m | 1 << bit for m in out]
    return out


def scatter_orders(num):
    bits = num.bit_length() - 1
    return ([0] + list(range(1, bits)), [0] + list(range(bits - 1, 0, -1)))


def scatter_plan(num):
    plan = []
    for order in scatter_orders(num):
        stages = []
        for t in range(len(order)):
            rest = order[t + 1 :]
            got = masks_over(rest)
            got.sort(key=lambda m: tuple(-(m >> b & 1) for b in rest))
            stages.append((order[t], got))
        plan.append(stages)
    return plan


def gather_plan(num):
    plan = []
    for order in scatter_orders(num):
        order = order[::-1]
        plan.append([(bit, masks_over(order[:t])) for t, bit in enumerate(order)])
    return plan


def split3(x):
    hi = x.astype(jnp.bfloat16)
    rest = x - hi.astype(jnp.float32)
    mid = rest.astype(jnp.bfloat16)
    low = (rest - mid.astype(jnp.float32)).astype(jnp.bfloat16)
    return hi, mid, low


def kernel(
    num,
    nblk,
    sample_count,
    snp_total,
    genotypes,
    pheno_row,
    fold_row,
    pheno_parts,
    fold_parts,
    table,
    perm,
    coeff_out,
    score_out,
    raw,
    dosage,
    gram,
    rs_buf,
    stat_buf,
    col_ref,
    target_ref,
    c1_ref,
    c2_ref,
    ld_hi,
    ld_lo,
    wt_ref,
    sel_buf,
    sel_recv,
    fin_samp,
    fin_blk,
    load_sem,
    rs_send,
    rs_recv,
    stat_send,
    stat_recv,
    ag_send,
    ag_recv,
    sel_send,
    sel_rsem,
    fin_send,
    fin_rsem,
    fbl_send,
    fbl_rsem,
):
    me = lax.axis_index("samp")
    zz = lax.axis_index("blk")
    num_rows, width = genotypes.shape
    rows = width // num
    half = width // 2
    loads = load_sem.shape[0]
    step = num_rows // loads

    def load(i):
        piece = pl.ds(i * step, step)
        return pltpu.make_async_copy(genotypes.at[piece, :], raw.at[piece, :], load_sem.at[i])

    for i in range(loads):
        load(i).start()

    barrier = pltpu.get_barrier_semaphore()
    for e in range(1, num):
        pl.semaphore_signal(barrier, inc=1, device_id={"samp": flip(me, e)}, device_id_type=MESH)
    for k in range(1, nblk):
        pl.semaphore_signal(
            barrier, inc=1, device_id={"blk": lax.rem(zz + k, nblk)}, device_id_type=MESH
        )
    pl.semaphore_wait(barrier, num - 1 + nblk - 1)

    plan = scatter_plan(num)
    slot_of = {}
    for h in range(2):
        for t, (_, got) in enumerate(plan[h]):
            for e in got:
                slot_of[h, t, e] = len(slot_of)

    def gram_block(e, h):
        return gram.at[flip(me, e), :, pl.ds(h * half, half)]

    def rs_copy(h, t, got):
        bit = plan[h][t][0]
        sent = got | 1 << bit
        src = gram_block(sent, h) if t == 0 else rs_buf.at[slot_of[h, t - 1, sent]]
        slot = slot_of[h, t, got]
        return pltpu.make_async_remote_copy(
            src_ref=src,
            dst_ref=rs_buf.at[slot],
            send_sem=rs_send.at[slot],
            recv_sem=rs_recv.at[slot],
            device_id={"samp": flip(me, 1 << bit)},
            device_id_type=MESH,
        )

    stages = len(plan[0])
    for i in range(loads):
        load(i).wait()
        dosage[i * step : (i + 1) * step, :] = raw[i * step : (i + 1) * step, :].astype(jnp.bfloat16)

    def rs_take(t, gots):
        for pos in range(len(gots[0])):
            for h in range(2):
                got = gots[h][pos]
                slot = slot_of[h, t, got]
                rs_copy(h, t, got).wait_recv()
                prev = gram_block(got, h) if t == 0 else rs_buf.at[slot_of[h, t - 1, got]]
                rs_buf[slot] = rs_buf[slot] + prev[...]
                if t + 1 < stages and got >> plan[h][t + 1][0] & 1:
                    rs_copy(h, t + 1, got & ~(1 << plan[h][t + 1][0])).start()

    unit = 1
    while unit * rows % 128 and unit * 2 <= num:
        unit *= 2

    def gram_unit(m):
        first = flip(me, m) // unit
        span = pl.ds(pl.multiple_of(first * (unit * rows), unit * rows), unit * rows)
        left = dosage[:, span].T
        for h in range(2):
            out = jnp.dot(
                left,
                dosage[:, h * half : (h + 1) * half],
                preferred_element_type=jnp.float32,
            )
            for j in range(unit):
                gram[first * unit + j, :, h * half : (h + 1) * half] = out[j * rows : (j + 1) * rows]
        for h in range(2):
            for got in plan[h][0][1]:
                if got // unit * unit == m:
                    rs_copy(h, 0, got).start()

    def unit_take(m):
        rs_take(0, [[got for got in plan[h][0][1] if got // unit * unit == m] for h in range(2)])

    units = [m for m in plan[0][0][1] if m % unit == 0]
    gram_unit(units[0])

    pheno = pheno_row[...]
    fold = fold_row[...]
    pieces = [jnp.ones(pheno.shape, jnp.bfloat16).astype(jnp.float32)]
    masked = [jnp.where(fold == k, pheno, 0.0) for k in range(FOLDS)]
    parts = [split3(x) for x in masked]
    for which in range(3):
        for k in range(FOLDS):
            pieces.append(parts[k][which].astype(jnp.float32))
    left = jnp.concatenate(pieces, axis=0).astype(jnp.bfloat16)
    geno = dosage[...]
    prod = jnp.dot(left, geno, preferred_element_type=jnp.float32)
    squares = jnp.dot(
        jnp.ones((16, geno.shape[0]), jnp.bfloat16), geno * geno, preferred_element_type=jnp.float32
    )
    lane = lax.broadcasted_iota(jnp.int32, (1, width), 1)
    extra = jnp.zeros((1, width), jnp.float32)
    for k in range(FOLDS):
        extra = jnp.where(lane == k, jnp.sum(masked[k], axis=1, keepdims=True), extra)
        count = jnp.sum(jnp.where(fold == k, 1.0, 0.0), axis=1, keepdims=True)
        extra = jnp.where(lane == 8 + k, count, extra)
    stat_buf[me] = jnp.concatenate(
        [
            prod[0:1],
            squares[0:1],
            (prod[1 + 2 * FOLDS : 1 + 3 * FOLDS] + prod[1 + FOLDS : 1 + 2 * FOLDS])
            + prod[1 : 1 + FOLDS],
            extra,
        ],
        axis=0,
    )

    def to_samp(buf, e, send, recv, holder):
        return pltpu.make_async_remote_copy(
            src_ref=buf.at[holder],
            dst_ref=buf.at[holder],
            send_sem=send.at[e - 1],
            recv_sem=recv.at[e - 1],
            device_id={"samp": flip(me, e)},
            device_id_type=MESH,
        )

    for e in range(1, num):
        to_samp(stat_buf, e, stat_send, stat_recv, me).start()

    for i in range(1, len(units)):
        gram_unit(units[i])
        unit_take(units[i - 1])
    unit_take(units[-1])

    for e in range(1, num):
        to_samp(stat_buf, e, stat_send, stat_recv, flip(me, e)).wait_recv()
    total = stat_buf[0]
    for d in range(1, num):
        total = total + stat_buf[d]
    mean_row = total[0:1] / sample_count
    scale_row = jnp.sqrt(total[1:2] / sample_count - mean_row * mean_row + epsilon)
    turned = total.T
    mean_col = turned[:, 0:1] / sample_count
    scale_col = jnp.sqrt(turned[:, 1:2] / sample_count - mean_col * mean_col + epsilon)
    col_ref[:, 0:1] = mean_col
    col_ref[:, 1:2] = scale_col
    fold_pheno = [total[7:8, k : k + 1] for k in range(FOLDS)]
    counts = [total[7:8, 8 + k : 9 + k] for k in range(FOLDS)]
    pheno_all = sum(fold_pheno[1:], fold_pheno[0])
    geno_pheno = [turned[:, 2 + k : 3 + k] for k in range(FOLDS)]
    geno_pheno_all = sum(geno_pheno[1:], geno_pheno[0])
    thresh = table[0:1, :]
    shrink = table[1:2, :]
    fold_of = table[2:3, :]
    target = jnp.zeros((width, GRID), jnp.float32)
    for k in range(FOLDS):
        z = (geno_pheno_all - geno_pheno[k] - (pheno_all - fold_pheno[k]) * mean_col) / (
            scale_col * jnp.sqrt(sample_count - counts[k])
        )
        target = jnp.where(fold_of == float(k), z, target)
    target_ref[...] = target
    c1_ref[...] = soft_threshold(step_size * target, thresh)

    for t in range(1, stages):
        rs_take(t, [plan[h][t][1] for h in range(2)])

    mine = pl.ds(pl.multiple_of(me * rows, rows), rows)
    mean_mine = col_ref[mine, 0:1]
    scale_mine = col_ref[mine, 1:2]
    for h in range(2):
        cols = slice(h * half, (h + 1) * half)
        summed = rs_buf[slot_of[h, stages - 1, 0]]
        block = (summed / sample_count - mean_mine * mean_row[:, cols]) / (
            scale_mine * scale_row[:, cols]
        )
        upper = block.astype(jnp.bfloat16)
        ld_hi[:, cols] = upper
        ld_lo[:, cols] = (block - upper.astype(jnp.float32)).astype(jnp.bfloat16)

    def sweep(full, out):
        held = full[mine, :]
        whole = full[...]
        upper = whole.astype(jnp.bfloat16)
        lower = (whole - upper.astype(jnp.float32)).astype(jnp.bfloat16)
        applied = (
            jnp.dot(ld_hi[...], lower, preferred_element_type=jnp.float32)
            + jnp.dot(ld_lo[...], upper, preferred_element_type=jnp.float32)
        ) + jnp.dot(ld_hi[...], upper, preferred_element_type=jnp.float32)
        gradient = (
            (1.0 - shrink) * applied
            + shrink * held
            - target_ref[mine, :]
        )
        out[mine, :] = soft_threshold(held - step_size * gradient, thresh)

    aplan = gather_plan(num)
    aslot = {}
    for h in range(2):
        for t, (_, held) in enumerate(aplan[h]):
            for e in held:
                aslot[h, t, e] = len(aslot)
    part = rows // 2

    def ag_copy(buf, which, h, t, e, owner):
        place = buf.at[pl.ds(pl.multiple_of(owner * rows + h * part, part), part), :]
        slot = aslot[h, t, e]
        return pltpu.make_async_remote_copy(
            src_ref=place,
            dst_ref=place,
            send_sem=ag_send.at[which, slot],
            recv_sem=ag_recv.at[which, slot],
            device_id={"samp": flip(me, 1 << aplan[h][t][0])},
            device_id_type=MESH,
        )

    def gather(buf, which):
        def arrived(h, first, e):
            for t in range(first, len(aplan[h])):
                ag_copy(buf, which, h, t, e, flip(me, e)).start()

        for h in range(2):
            arrived(h, 0, 0)
        for t in range(len(aplan[0])):
            for pos in range(len(aplan[0][t][1])):
                for h in range(2):
                    bit, held = aplan[h][t]
                    e = held[pos]
                    got = e | 1 << bit
                    ag_copy(buf, which, h, t, e, flip(me, got)).wait_recv()
                    arrived(h, t + 1, got)

    def gather_end(buf, which):
        for h in range(2):
            for t, (_, held) in enumerate(aplan[h]):
                for e in held:
                    ag_copy(buf, which, h, t, e, flip(me, e)).wait_send()

    sweep(c1_ref, c2_ref)
    gather(c2_ref, 0)
    sweep(c2_ref, coeff_out)
    gather(coeff_out, 1)

    weighted = (coeff_out[...] / col_ref[:, 1:2]).astype(jnp.bfloat16)
    turned_w = lax.dot_general(
        perm[...], weighted, (((1,), (1,)), ((), ())), preferred_element_type=jnp.float32
    )
    wt_ref[...] = turned_w.astype(jnp.bfloat16)
    offset = jnp.sum(turned_w * mean_row, axis=1, keepdims=True)

    people = fold_parts.shape[2]

    def sel_copy(k):
        return pltpu.make_async_remote_copy(
            src_ref=sel_buf.at[k],
            dst_ref=sel_recv.at[k - 1],
            send_sem=sel_send.at[k - 1],
            recv_sem=sel_rsem.at[k - 1],
            device_id={"blk": lax.rem(zz + k, nblk)},
            device_id_type=MESH,
        )

    for k in list(range(1, nblk)) + [0]:
        peer = lax.rem(zz + k, nblk)
        some = dosage[pl.ds(pl.multiple_of(peer * people, people), people), :]
        value = (
            lax.dot_general(
                wt_ref[...], some, (((1,), (1,)), ((), ())), preferred_element_type=jnp.float32
            )
            - offset
        )
        ids = fold_parts[peer]
        chosen = jnp.zeros((PER_FOLD, people), jnp.float32)
        for f in range(FOLDS):
            chosen = jnp.where(ids == f, value[f * PER_FOLD : (f + 1) * PER_FOLD], chosen)
        sel_buf[k] = chosen
        if k:
            sel_copy(k).start()
    predicted = sel_buf[0]
    for k in range(1, nblk):
        sel_copy(k).wait_recv()
        predicted = predicted + sel_recv[k - 1]
    predicted = predicted / math.sqrt(snp_total)
    ids = fold_parts[zz]
    in_fold = lax.broadcasted_iota(jnp.int32, (8, people), 0) == ids
    lanes = (((1,), (1,)), ((), ()))
    numer = lax.dot_general(
        jnp.where(in_fold, pheno_parts[zz], 0.0),
        predicted,
        lanes,
        precision=highest,
        preferred_element_type=jnp.float32,
    )
    denom = lax.dot_general(
        jnp.where(in_fold, 1.0, 0.0),
        predicted * predicted,
        lanes,
        precision=highest,
        preferred_element_type=jnp.float32,
    )
    both = jnp.concatenate([numer, denom], axis=0)
    fin_samp[me] = jnp.concatenate(
        [both, jnp.zeros((16, fin_samp.shape[2] - PER_FOLD), jnp.float32)], axis=1
    )
    for e in range(1, num):
        to_samp(fin_samp, e, fin_send, fin_rsem, me).start()
    for e in range(1, num):
        to_samp(fin_samp, e, fin_send, fin_rsem, flip(me, e)).wait_recv()
    both = fin_samp[0]
    for d in range(1, num):
        both = both + fin_samp[d]
    fin_blk[zz] = both

    def fbl_copy(k, holder):
        return pltpu.make_async_remote_copy(
            src_ref=fin_blk.at[holder],
            dst_ref=fin_blk.at[holder],
            send_sem=fbl_send.at[k - 1],
            recv_sem=fbl_rsem.at[k - 1],
            device_id={"blk": lax.rem(zz + k, nblk)},
            device_id_type=MESH,
        )

    for k in range(1, nblk):
        fbl_copy(k, zz).start()
    for k in range(1, nblk):
        fbl_copy(k, lax.rem(zz + nblk - k, nblk)).wait_recv()
    both = fin_blk[0]
    for d in range(1, nblk):
        both = both + fin_blk[d]
    row = lax.broadcasted_iota(jnp.int32, (16, 1), 0)
    count_col = jnp.ones((16, 1), jnp.float32)
    for k in range(FOLDS):
        count_col = jnp.where((row == k) | (row == 8 + k), counts[k], count_col)
    score_out[...] = both / count_col

    for h in range(2):
        for t in range(stages):
            for got in plan[h][t][1]:
                rs_copy(h, t, got).wait_send()
    for e in range(1, num):
        to_samp(stat_buf, e, stat_send, stat_recv, me).wait_send()
        to_samp(fin_samp, e, fin_send, fin_rsem, me).wait_send()
    gather_end(c2_ref, 0)
    gather_end(coeff_out, 1)
    for k in range(1, nblk):
        sel_copy(k).wait_send()
        fbl_copy(k, zz).wait_send()


def local(genotypes, phenotype, fold_ids):
    num_rows, width = genotypes.shape
    num = lax.axis_size("samp")
    nblk = lax.axis_size("blk")
    people = num_rows // nblk
    rows = width // num
    fold_of, penalty, shrink = grid_tables()
    zero = np.zeros(GRID)
    table = jnp.asarray(
        np.stack([step_size * penalty, shrink, fold_of] + [zero] * 5).astype(np.float32)
    )
    order = np.arange(GRID)
    perm = jnp.asarray(
        ((order % PER_FOLD * FOLDS + order // PER_FOLD)[:, None] == order[None, :]).astype(
            jnp.bfloat16
        )
    )
    rs_slots = 2 * (num - 1)
    ag_slots = 2 * (num - 1)
    dma = pltpu.SemaphoreType.DMA
    f32 = jnp.float32
    coeff_all, scores = pl.pallas_call(
        functools.partial(kernel, num, nblk, num_rows * num, width * nblk),
        out_shape=(
            jax.ShapeDtypeStruct((width, GRID), f32),
            jax.ShapeDtypeStruct((16, 128), f32),
        ),
        in_specs=[pl.BlockSpec(memory_space=pl.ANY)]
        + [pl.BlockSpec(memory_space=pltpu.VMEM)] * 6,
        out_specs=(pl.BlockSpec(memory_space=pltpu.VMEM),) * 2,
        scratch_shapes=[
            pltpu.VMEM((num_rows, width), jnp.int32),
            pltpu.VMEM((num_rows, width), jnp.bfloat16),
            pltpu.VMEM((num, rows, width), f32),
            pltpu.VMEM((rs_slots, rows, width // 2), f32),
            pltpu.VMEM((num, 8, width), f32),
            pltpu.VMEM((width, 8), f32),
            pltpu.VMEM((width, GRID), f32),
            pltpu.VMEM((width, GRID), f32),
            pltpu.VMEM((width, GRID), f32),
            pltpu.VMEM((rows, width), jnp.bfloat16),
            pltpu.VMEM((rows, width), jnp.bfloat16),
            pltpu.VMEM((GRID, width), jnp.bfloat16),
            pltpu.VMEM((nblk, PER_FOLD, people), f32),
            pltpu.VMEM((nblk - 1, PER_FOLD, people), f32),
            pltpu.VMEM((num, 16, 128), f32),
            pltpu.VMEM((nblk, 16, 128), f32),
            dma((8,)),
            dma((rs_slots,)),
            dma((rs_slots,)),
            dma((num - 1,)),
            dma((num - 1,)),
            dma((2, ag_slots)),
            dma((2, ag_slots)),
            dma((nblk - 1,)),
            dma((nblk - 1,)),
            dma((num - 1,)),
            dma((num - 1,)),
            dma((nblk - 1,)),
            dma((nblk - 1,)),
        ],
        compiler_params=pltpu.CompilerParams(
            collective_id=0, has_side_effects=True, vmem_limit_bytes=62 * 1024 * 1024
        ),
    )(
        genotypes,
        phenotype.reshape(1, num_rows),
        fold_ids.reshape(1, num_rows),
        phenotype.reshape(nblk, 1, people),
        fold_ids.reshape(nblk, 1, people),
        table,
        perm,
    )
    scores = scores.reshape(2, 8, 128)[:, :FOLDS, :PER_FOLD]
    return (coeff_all, scores.transpose(0, 2, 1).reshape(2, GRID))


def solution(mesh):
    return jax.shard_map(
        local,
        mesh=mesh,
        in_specs=(P("samp", "blk"), P("samp"), P("samp")),
        out_specs=(P("blk", None), P()),
        check_vma=False,
    )
```
